32 devices in a mesh: sub: 8 (over y, x, core), tm: 4 (over z).
Axes of the slice: x: 2, y: 2, z: 4, core: 2. Of those that a mesh axis runs over, the one named last changes fastest.
Arguments:
- voltages: bfloat16 [8192, 12, 2, 2048], P('sub', 'tm'), may hold values from -6 to 6
- slot_feed: int32 [2048], replicated, may hold values from 0 to 2047, each once
- chan_lag: int32 [8192], replicated, may hold values from 0 to 4096
- trial_dm: int32 [512], replicated, may hold values from 0 to 4096
- beam_order: int32 [1024], replicated, may hold values from 0 to 1023, each once
Outputs:
- dedispersed: float32 [1024, 12, 512], P('sub', 'tm')
The draws below stay inside these ranges and needn't reach their ends.
Inputs may be any that keep to these rules, and one draw needn't show every extreme that they name: `slot_feed`: each feed once; slot (p * 4 + y) * 256 + n is polarization p at east-west position y and north-south position n. `beam_order`: each beam once.
All inputs are finite; a program needn't handle non-finite values.
Results may differ from the reference program's by a relative error of at most 0.00088.
Values may be sent and summed in bfloat16 or wider, within the bound.
No kernel may reach another device: no remote copies, remote signals or barrier semaphores. Data moves between devices by JAX's collectives and lax.ppermute only.
A program may use at most 192 MiB of HBM per device.

```python
import math
import jax
import jax.numpy as jnp
from jax import lax

NS = 256
CYL = 4
POL = 2
CHANNELS = 8192
NDM = 512
MAXD = 6
LAG_TOP = 4096
FEEDS = 2048
BEAMS = 1024
TIME = 12
QUANT = 2796202


def shuffled_ramp(key, length):
    increments = jax.random.randint(jax.random.fold_in(key, 3), (length,), 1, 4).astype(jnp.int32)
    running = jnp.cumsum(increments).astype(jnp.int32)
    lowest = running[0]
    highest = running[length - 1]
    ramp = ((running - lowest) * LAG_TOP // (highest - lowest)).astype(jnp.int32)
    return jax.random.permutation(jax.random.fold_in(key, 5), ramp).astype(jnp.int32)


def draw_chan_lag(key, part):
    return shuffled_ramp(jax.random.fold_in(key, 11), CHANNELS)


def draw_trial_dm(key, part):
    return shuffled_ramp(jax.random.fold_in(key, 23), NDM)


def levels(stream_key, dims, pieces, smallest, high):
    factor_of = 1.0
    for axis_at, shards_of in pieces:
        steps = jax.random.uniform(jax.random.fold_in(jax.random.fold_in(stream_key, 6), axis_at), (shards_of,), jnp.float32, smallest / len(pieces), high / len(pieces))
        factor_of = factor_of * jnp.repeat(jnp.exp(steps), dims[axis_at] // shards_of).reshape((-1,) + (1,) * (len(dims) - 1 - axis_at))
    return factor_of


def gaussian(rng, dims, deviation, most, pieces=(), kind=jnp.bfloat16):
    level = levels(rng, dims, pieces, -0.22, 0.18) if pieces else 1.0
    array = jax.random.normal(rng, dims, jnp.float32) * deviation * level
    return jnp.minimum(jnp.maximum(array, -most), most).astype(kind)


def setup_inputs(seed: int = 0) -> dict:
    splits = jax.random.split(jax.random.key(seed), 6)
    return {
        "voltages": gaussian(splits[0], (CHANNELS, TIME, 2, FEEDS), 1.0, 6.0, ((0, 8), (1, 4))),
        "slot_feed": jax.random.permutation(splits[1], FEEDS).astype(jnp.int32),
        "chan_lag": draw_chan_lag(jax.random.fold_in(splits[5], 71), 0),
        "trial_dm": draw_trial_dm(jax.random.fold_in(splits[5], 71), 0),
        "beam_order": jax.random.permutation(splits[4], BEAMS).astype(jnp.int32),
    }


def north_table():
    positions = jnp.arange(NS, dtype=jnp.int32)
    phase_index = positions[:, None] * positions[None, :] % NS
    angles = phase_index.astype(jnp.float32) * (2.0 * math.pi / NS)
    cosine = jnp.cos(angles) / math.sqrt(NS)
    sine_part = jnp.sin(angles) / math.sqrt(NS)
    real_row = jnp.stack([cosine, -sine_part], axis=1)
    imag_row = jnp.stack([sine_part, cosine], axis=1)
    return jnp.stack([real_row, imag_row], axis=0).astype(jnp.bfloat16)

def west_table():
    cylinder = jnp.arange(CYL, dtype=jnp.int32)
    quarter_turn = cylinder[:, None] * cylinder[None, :] % 4
    cosine = (quarter_turn == 0).astype(jnp.float32) - (quarter_turn == 2).astype(jnp.float32)
    sine_part = (quarter_turn == 1).astype(jnp.float32) - (quarter_turn == 3).astype(jnp.float32)
    real_row = jnp.stack([cosine, -sine_part], axis=2)
    imag_row = jnp.stack([sine_part, cosine], axis=2)
    return 0.5 * jnp.stack([real_row, imag_row], axis=1)

def compute_power(north_beams):
    west_beams = jnp.einsum('ctpyom,yoeq->ctpeqm', north_beams, west_table(), precision=lax.Precision.HIGHEST)
    squares = lax.optimization_barrier(jnp.sum(west_beams * west_beams, axis=(2, 4)))
    return squares.reshape(north_beams.shape[0], north_beams.shape[1], CYL * NS)

def delay_table(lag_rows, trial_dm):
    return (lag_rows[:, None] * trial_dm[None, :] // QUANT).astype(jnp.int32)

def reference(voltages, slot_feed, chan_lag, trial_dm, beam_order):
    width = 64
    blocks = CHANNELS // width
    samples = voltages.shape[1]
    table = north_table().astype(jnp.float32)

    def accumulate(accumulated, inputs):
        volt_block, lag_rows = inputs
        grid_volts = jnp.take(volt_block, slot_feed, axis=3).reshape(width, samples, 2, POL, CYL, NS)
        north_beams = jnp.einsum('ctrpyn,rnom->ctpyom', grid_volts.astype(jnp.float32), table, precision=lax.Precision.HIGHEST)
        intensity = compute_power(north_beams)
        ordered = jnp.take(intensity, beam_order, axis=2)
        average = lax.optimization_barrier(jnp.sum(ordered, axis=1)) / samples
        normal = (ordered - average[:, None, :]).astype(jnp.bfloat16)
        source = normal.astype(jnp.float32)
        delays = delay_table(lag_rows, trial_dm)
        for delay_step in range(MAXD + 1):
            onehot = (delays == delay_step).astype(jnp.float32)
            part = jnp.einsum('ctb,cd->btd', source, onehot, precision=lax.Precision.HIGHEST)
            moved = jnp.pad(part, ((0, 0), (delay_step, 0), (0, 0)))[:, :samples, :]
            accumulated = accumulated + moved
        return (accumulated, None)
    initial = jnp.zeros((BEAMS, samples, NDM), jnp.float32)
    accumulated, ignored = lax.scan(accumulate, initial, (voltages.reshape(blocks, width, samples, 2, FEEDS), chan_lag.reshape(blocks, width)))
    return accumulated / math.sqrt(CHANNELS)
```

```python
import functools
import math

import jax
import jax.numpy as jnp
from jax import lax
from jax.experimental import pallas as pl
from jax.experimental.pallas import tpu as pltpu
from jax.sharding import PartitionSpec as P
import numpy as np

NS = 256
CYL = 4
POL = 2
MAXD = 6
QUANT = 2796202
HALF = NS // 2
LANES = 128
SPLIT = (3, 3, 2)
GROUPS = (2,)


def vmem(mib):
    return pltpu.CompilerParams(vmem_limit_bytes=mib << 20)


def matrix_kernel(slot_ref, table_ref, out_ref):
    rows = out_ref.shape[0]
    feed = pl.program_id(0) * rows + lax.broadcasted_iota(jnp.int32, (rows, NS), 0)
    first = lax.broadcasted_iota(jnp.int32, (rows, HALF), 1) == 0
    pick = [
        jnp.where(slot_ref[:, i * NS : (i + 1) * NS] == feed, 1.0, 0.0).astype(jnp.bfloat16)
        for i in range(POL * CYL)
    ]
    waves = jnp.dot(
        jnp.concatenate(pick, axis=0), table_ref[...], preferred_element_type=jnp.float32
    )
    for p in range(POL):
        both = [waves[(p * CYL + y) * rows : (p * CYL + y + 1) * rows] for y in range(CYL)]
        cosine = [v[:, :NS] for v in both]
        sine = [v[:, NS:] for v in both]
        even_cos, odd_cos = cosine[0] + cosine[2], cosine[1] + cosine[3]
        even_sin, odd_sin = sine[0] + sine[2], sine[1] + sine[3]
        real_one = (cosine[0] - cosine[2]) - (sine[1] - sine[3])
        imag_one = (sine[2] - sine[0]) - (cosine[1] - cosine[3])
        blocks = [
            (real_one[:, :HALF], imag_one[:, :HALF]),
            (real_one[:, HALF:], imag_one[:, HALF:]),
        ]
        for cos_sum, sin_sum in (
            (even_cos + odd_cos, even_sin + odd_sin),
            (even_cos - odd_cos, even_sin - odd_sin),
        ):
            imag = jnp.where(first, cos_sum[:, HALF:], -sin_sum[:, :HALF])
            blocks.append((cos_sum[:, :HALF], imag))
        for h, pair in enumerate(blocks):
            for i in range(2):
                at = h * 512 + p * 256 + i * LANES
                out_ref[:, at : at + LANES] = pair[i].astype(jnp.bfloat16)


def beam_matrix(slot_feed):
    feeds = slot_feed.shape[0]
    steps = np.arange(NS)
    angles = (steps[:, None] * steps[None, :] % NS).astype(np.float32) * np.float32(2.0 * math.pi / NS)
    wave = np.concatenate([np.cos(angles), np.sin(angles)], axis=1) / np.float32(math.sqrt(NS))
    table = jnp.asarray(wave).astype(jnp.bfloat16) * jnp.bfloat16(0.5)
    rows = 256
    return pl.pallas_call(
        matrix_kernel,
        grid=(feeds // rows,),
        in_specs=[
            pl.BlockSpec((1, feeds), lambda i: (0, 0)),
            pl.BlockSpec((NS, 2 * NS), lambda i: (0, 0)),
        ],
        out_specs=pl.BlockSpec((rows, 2 * CYL * NS), lambda i: (i, 0)),
        out_shape=jax.ShapeDtypeStruct((feeds, 2 * CYL * NS), jnp.bfloat16),
        compiler_params=vmem(60),
        name="matrix",
    )(slot_feed.reshape(1, feeds), table)


def beam_place(beam):
    east, north = beam // NS, beam % NS
    mirror = (NS - north) % NS
    one = (north // HALF) * NS + north % HALF
    three = (mirror // HALF) * NS + HALF + mirror % HALF
    even = jnp.where(north < HALF, north, HALF + jnp.where(north == HALF, 0, mirror))
    even = even + 2 * NS + (east // 2) * NS
    return jnp.where(east == 1, one, jnp.where(east == 3, three, even))


def form_kernel(token_ref, volts_ref, matrix_ref, power_ref, total_ref, code_ref, held, scratch, arrived, *, rows, samples):
    copies = []
    for h in range(4):
        columns = pl.ds(h * 512, 512)
        copies.append(
            pltpu.make_async_copy(matrix_ref.at[:, columns], held.at[:, columns], arrived.at[h])
        )

    @pl.when(pl.program_id(0) == 0)
    def _():
        for copy in copies:
            copy.start()

    @pl.when(pl.program_id(0) == 0)
    def _():
        for copy in copies:
            copy.wait()

    for h in range(4):
        product = jnp.dot(
            volts_ref[...].reshape(rows * samples * 2, volts_ref.shape[3]),
            held[:, h * 512 : (h + 1) * 512],
            preferred_element_type=jnp.float32,
        )
        slot = h % 2
        for part in range(4):
            scratch[slot, part] = product[:, part * LANES : (part + 1) * LANES]
        both_real = lax.broadcasted_iota(jnp.int32, (rows, LANES), 1) == 0
        sums = [None, None]
        for t in range(samples):
            pair = [None, None]
            for p in range(POL):

                def part(r, i):
                    return scratch[slot, 2 * p + i, pl.ds(2 * t + r, rows, stride=2 * samples), :]

                r0, r1, i0, i1 = part(0, 0), part(1, 0), part(0, 1), part(1, 1)
                rr = r0 * r0 + r1 * r1
                ii = i0 * i0 + i1 * i1
                cross = 2.0 * (i0 * r1 - r0 * i1)
                if h < 2:
                    here, there = rr + (ii + cross), ii + (rr - cross)
                else:
                    here = rr + jnp.where(both_real, 0.0, ii + cross)
                    there = ii + jnp.where(both_real, 0.0, rr - cross)
                pair = [v if u is None else u + v for u, v in zip(pair, (here, there))]
            for s in range(2):
                power_ref[t, :, h * 256 + s * LANES : h * 256 + (s + 1) * LANES] = pair[s]
                sums[s] = pair[s] if sums[s] is None else sums[s] + pair[s]
        for s in range(2):
            total_ref[:, h * 256 + s * LANES : h * 256 + (s + 1) * LANES] = sums[s]
    encode(total_ref[...], code_ref)


def encode(value, code_ref):
    width = value.shape[1]
    largest = jnp.maximum(jnp.max(value, axis=1, keepdims=True), 1e-30)
    power = jnp.floor(jnp.log(largest) * (64.0 / math.log(2.0))) + 1.0
    inverse = jnp.exp(power * (-math.log(2.0) / 64.0)) * 65535.0
    level = jnp.minimum(jnp.floor(value * inverse + 0.5), 65535.0)
    code_ref[:, :width] = (level.astype(jnp.int32) - 32768).astype(jnp.int16)
    lanes = jnp.broadcast_to(power, (value.shape[0], LANES))
    code_ref[:, width:] = lanes.astype(jnp.int32).astype(jnp.int16)


def decode(code_ref):
    width = code_ref.shape[1] - LANES
    power = code_ref[:, width:].astype(jnp.int32).astype(jnp.float32)[:, 0:1]
    scale = jnp.exp(power * (math.log(2.0) / 64.0)) / 65535.0
    return (code_ref[:, :width].astype(jnp.int32) + 32768).astype(jnp.float32) * scale


def form(token, voltages, matrix, first, count):
    samples, feeds = voltages.shape[1], voltages.shape[3]
    beams = CYL * NS
    rows = math.gcd(128, count)
    start = first // rows
    return pl.pallas_call(
        functools.partial(form_kernel, rows=rows, samples=samples),
        grid=(count // rows,),
        in_specs=[
            pl.BlockSpec((8, LANES), lambda i: (0, 0)),
            pl.BlockSpec((rows, samples, 2, feeds), lambda i: (start + i, 0, 0, 0)),
            pl.BlockSpec(memory_space=pl.ANY),
        ],
        out_specs=[
            pl.BlockSpec((samples, rows, beams), lambda i: (0, i, 0)),
            pl.BlockSpec((rows, beams), lambda i: (i, 0)),
            pl.BlockSpec((rows, beams + LANES), lambda i: (i, 0)),
        ],
        out_shape=[
            jax.ShapeDtypeStruct((samples, count, beams), jnp.float32),
            jax.ShapeDtypeStruct((count, beams), jnp.float32),
            jax.ShapeDtypeStruct((count, beams + LANES), jnp.int16),
        ],
        scratch_shapes=[
            pltpu.VMEM((feeds, 2 * beams), jnp.bfloat16),
            pltpu.VMEM((2, 4, rows * samples * 2, LANES), jnp.float32),
            pltpu.SemaphoreType.DMA((4,)),
        ],
        compiler_params=vmem(60),
        name="form",
    )(token, voltages, matrix)


def collect(flags_ref, local_ref, codes):
    total = local_ref[...]
    for i, code in enumerate(codes):
        total = total + jnp.where(flags_ref[i : i + 1, 0:1] != 0, decode(code), 0.0)
    return total


def hop_kernel(flags_ref, local_ref, *refs):
    encode(collect(flags_ref, local_ref, refs[:-1]), refs[-1])


def hop(flags, local, codes):
    count, beams = local.shape
    rows = math.gcd(128, count)
    wide = pl.BlockSpec((rows, beams + LANES), lambda i: (i, 0))
    return pl.pallas_call(
        hop_kernel,
        grid=(count // rows,),
        in_specs=[
            pl.BlockSpec((8, LANES), lambda i: (0, 0)),
            pl.BlockSpec((rows, beams), lambda i: (i, 0)),
        ]
        + [wide] * len(codes),
        out_specs=wide,
        out_shape=jax.ShapeDtypeStruct((count, beams + LANES), jnp.int16),
        compiler_params=vmem(60),
        name="hop",
    )(flags, local, *codes)


def norm_kernel(flags_ref, power_ref, local_ref, *refs, gathered, samples, groups, scale):
    gather, spread, (order_ref, out_ref) = refs[:gathered], refs[gathered:-2], refs[-2:]
    total = collect(flags_ref, local_ref, gather)
    for i, code in enumerate(spread):
        at = gathered + i
        total = jnp.where(flags_ref[at : at + 1, 0:1] != 0, decode(code), total)
    average = total * (1.0 / scale)
    order = order_ref[...]
    size, rows = order.shape[0] // groups, average.shape[0]
    normal = [(power_ref[t] - average).astype(jnp.bfloat16) for t in range(samples)]
    moved = lax.dot_general(
        order,
        jnp.concatenate(normal, axis=0),
        (((1,), (1,)), ((), ())),
        preferred_element_type=jnp.float32,
    ).astype(jnp.bfloat16)
    for t in range(samples):
        for g in range(groups):
            out_ref[g, t] = moved[g * size : (g + 1) * size, t * rows : (t + 1) * rows]


def normalize(flags, power, local, gather, spread, order, groups, scale):
    samples, count, beams = power.shape
    rows = 256 if count % 256 == 0 else count
    size = beams // groups
    wide = pl.BlockSpec((rows, beams + LANES), lambda i: (i, 0))
    return pl.pallas_call(
        functools.partial(
            norm_kernel, gathered=len(gather), samples=samples, groups=groups, scale=scale
        ),
        grid=(count // rows,),
        in_specs=[
            pl.BlockSpec((8, LANES), lambda i: (0, 0)),
            pl.BlockSpec((samples, rows, beams), lambda i: (0, i, 0)),
            pl.BlockSpec((rows, beams), lambda i: (i, 0)),
        ]
        + [wide] * (len(gather) + len(spread))
        + [pl.BlockSpec((beams, beams), lambda i: (0, 0))],
        out_specs=pl.BlockSpec((groups, samples, size, rows), lambda i: (0, 0, 0, i)),
        out_shape=jax.ShapeDtypeStruct((groups, samples, size, count), jnp.bfloat16),
        compiler_params=vmem(60),
        name="norm",
    )(flags, power, local, *gather, *spread, order)


def sum_kernel(lag_ref, trial_ref, *refs, parts, samples, reach, resume, final):
    blocks, refs = refs[:parts], refs[parts:]
    if resume:
        (old_sums, old_whole), refs = refs[:2], refs[2:]
    if final:
        out_ref, late_ref, sums, whole = refs
    else:
        sums, whole = refs
    step = pl.program_id(0)

    @pl.when(step == 0)
    def _():
        sums[...] = old_sums[...] if resume else jnp.zeros_like(sums)
        whole[...] = old_whole[...] if resume else jnp.zeros_like(whole)

    size = blocks[0].shape[2]
    lots = blocks[0].shape[0]
    source = [b[g].reshape(samples * size, b.shape[3]) for g in range(lots) for b in blocks]
    source = source[0] if len(source) == 1 else jnp.concatenate(source, axis=1)
    lag = [lag_ref[g] for g in range(lots)]
    lag = lag[0] if lots == 1 else jnp.concatenate(lag, axis=1)
    product = trial_ref[:, 0:1] * lag
    for k in range(1, reach + 1):
        late = jnp.where(product >= float(k * QUANT), 1.0, 0.0).astype(jnp.bfloat16)
        sums[k - 1] += lax.dot_general(
            source, late, (((1,), (1,)), ((), ())), preferred_element_type=jnp.float32
        )
    wide = source.astype(jnp.float32)
    whole[...] += sum(wide[:, i : i + LANES] for i in range(0, wide.shape[1], LANES))
    if not final:
        return

    @pl.when(step == pl.num_programs(0) - 1)
    def _():
        first = jnp.sum(whole[...], axis=1, keepdims=True)

        def level(k, t):
            rows = slice(t * size, (t + 1) * size)
            if k == 0:
                return jnp.broadcast_to(first[rows], (size, sums.shape[2]))
            return sums[k - 1, rows]

        for row in range(samples + reach):
            value = None
            for t in range(samples):
                k = row - t
                if 0 <= k <= reach:
                    piece = level(k, t) if k == reach else level(k, t) - level(k + 1, t)
                    value = piece if value is None else value + piece
            if row < samples:
                out_ref[row] = value
            else:
                encode_signed(value, late_ref, row - samples)


def encode_signed(value, code_ref, row):
    width = value.shape[1]
    largest = jnp.maximum(jnp.max(jnp.abs(value), axis=1, keepdims=True), 1e-30)
    power = jnp.floor(jnp.log(largest) * (64.0 / math.log(2.0))) + 1.0
    inverse = jnp.exp(power * (-math.log(2.0) / 64.0)) * 32767.0
    level = jnp.clip(jnp.floor(value * inverse + 0.5), -32767.0, 32767.0)
    code_ref[row, :, :width] = level.astype(jnp.int32).astype(jnp.int16)
    lanes = jnp.broadcast_to(power, (value.shape[0], LANES))
    code_ref[row, :, width:] = lanes.astype(jnp.int32).astype(jnp.int16)


def decode_signed(code):
    scale = jnp.exp(code[:, :, -1:].astype(jnp.float32) * (math.log(2.0) / 64.0)) / 32767.0
    return code[:, :, :-LANES].astype(jnp.float32) * scale


def sum_shifted(blocks, lag, trial, state, final):
    groups, samples, size, _ = blocks[0].shape
    trials, depth = trial.shape[0], lag.shape[2]
    lots = max(n for n in (1, 2, 4) if groups % n == 0 and (n == 1 or n * depth <= 1024))
    sums = jax.ShapeDtypeStruct((MAXD, samples * size, trials), jnp.float32)
    whole = jax.ShapeDtypeStruct((samples * size, LANES), jnp.float32)
    rows = jax.ShapeDtypeStruct((samples, size, trials), jnp.float32)
    late = jax.ShapeDtypeStruct((MAXD, size, trials + LANES), jnp.int16)
    outs = [rows, late] if final else [sums, whole]

    def fixed(shape):
        return pl.BlockSpec(shape, lambda i: (0,) * len(shape))

    return pl.pallas_call(
        functools.partial(
            sum_kernel,
            parts=len(blocks),
            samples=samples,
            reach=MAXD,
            resume=state is not None,
            final=final,
        ),
        grid=(groups // lots,),
        in_specs=[pl.BlockSpec((lots, 1, depth), lambda i: (i, 0, 0)), fixed(trial.shape)]
        + [pl.BlockSpec((lots,) + b.shape[1:], lambda i: (i, 0, 0, 0)) for b in blocks]
        + ([] if state is None else [fixed(v.shape) for v in state]),
        out_specs=[fixed(v.shape) for v in outs],
        out_shape=outs,
        scratch_shapes=[pltpu.VMEM(v.shape, v.dtype) for v in (sums, whole)] if final else [],
        compiler_params=vmem(60),
        name="shift_sum",
    )(lag, trial, *blocks, *(state or ()))


def hop_plan(shards, place):
    last, half = shards - 1, shards // 2
    far = jnp.minimum(place, last - place)
    gather = [[(s, s + 1), (last - s, last - s - 1)] for s in range(half - 1)]
    gather_flags = [far == s + 1 for s in range(half - 1)]
    if shards > 1:
        gather.append([(half - 1, half), (half, half - 1)])
        gather_flags.append(far == half - 1)
    spread = [[(s + 1, s), (last - s - 1, last - s)] for s in reversed(range(half - 1))]
    spread_flags = [far == s for s in reversed(range(half - 1))]
    flags = jnp.stack(gather_flags + spread_flags).astype(jnp.int32)
    flags = jnp.pad(flags, (0, 8 - flags.shape[0]))
    flags = jnp.broadcast_to(flags[:, None], (8, LANES))
    return gather, spread, flags


def after(value, *tokens):
    return lax.optimization_barrier((value, *tokens))[0]


def shifted(value, axis, steps):
    count = lax.axis_size(axis)
    return lax.ppermute(value, axis, [(s, s + steps) for s in range(count - steps)])


def per_device(voltages, slot_feed, chan_lag, trial_dm, beam_order):
    channels, samples = voltages.shape[:2]
    groups, shards = lax.axis_size("sub"), lax.axis_size("tm")
    beams = beam_order.shape[0]
    matrix = beam_matrix(slot_feed)
    order = (beam_place(beam_order)[:, None] == jnp.arange(beams)[None, :]).astype(jnp.bfloat16)
    lag = chan_lag.astype(jnp.float32).reshape(groups, 1, channels)
    trial = jnp.broadcast_to(trial_dm.astype(jnp.float32)[:, None], (trial_dm.shape[0], LANES))
    lag = chan_lag.astype(jnp.float32).reshape(groups, 1, channels)
    trial = jnp.broadcast_to(trial_dm.astype(jnp.float32)[:, None], (trial_dm.shape[0], LANES))
    gather, spread, flags = hop_plan(shards, lax.axis_index("tm"))
    hops = gather + spread
    eighth = channels // 8
    if eighth % LANES:
        counts = [LANES] * (channels // LANES)
    else:
        counts = [part * eighth for part in SPLIT]
    chunks = len(counts)
    starts = [sum(counts[:i]) for i in range(chunks + 1)]
    power, local, codes, blocks = {}, {}, {}, {}
    token, state, begin = matrix, None, 0
    for step in range(chunks + len(hops) + 2):
        if step < chunks:
            power[step], local[step], token = form(
                flags, voltages, after(matrix, token), starts[step], counts[step]
            )
            codes[step] = [lax.ppermute(token, "tm", hops[0])]
        for stage in range(1, len(hops)):
            i = step - stage
            if 0 <= i < chunks:
                received = codes[i]
                if stage <= len(gather):
                    token = hop(flags, after(local[i], token), received)
                else:
                    token = received[-1]
                received.append(lax.ppermute(token, "tm", hops[stage]))
        i = step - len(hops)
        if 0 <= i < chunks:
            moved = normalize(
                flags,
                after(power[i], token),
                local[i],
                codes[i][: len(gather)],
                codes[i][len(gather) :],
                order,
                groups,
                float(samples * shards),
            )
            token = moved
            if i:
                moved, blocks[i - 1] = lax.optimization_barrier((moved, blocks[i - 1]))
            blocks[i] = lax.all_to_all(moved, "sub", 0, 0, tiled=True)
        i = step - len(hops) - 1
        if i + 1 in GROUPS and i + 1 < chunks:
            part = [blocks[j] for j in range(begin, i + 1)]
            columns = after(lag[:, :, starts[begin] : starts[i + 1]], token)
            state = sum_shifted(part, columns, trial, state, False)
            token, begin = state[1], i + 1
    part = [blocks[j] for j in range(begin, chunks)]
    kept, late = sum_shifted(part, after(lag[:, :, starts[begin] :], token), trial, state, True)
    for distance in range(1, min(shards - 1, (MAXD + samples - 1) // samples) + 1):
        first = (distance - 1) * samples
        last = min(first + samples, MAXD)
        carried = decode_signed(shifted(late[first:last], "tm", distance))
        kept = kept + jnp.pad(carried, ((0, samples - (last - first)), (0, 0), (0, 0)))
    return jnp.transpose(kept, (1, 0, 2)) / math.sqrt(chan_lag.shape[0])


def solution(mesh):
    return jax.shard_map(
        per_device,
        mesh=mesh,
        in_specs=(P("sub", "tm", None, None), P(), P(), P(), P()),
        out_specs=P("sub", "tm", None),
        check_vma=False,
    )
```
